512 devices in a mesh: dp: 8 (over z), seq: 64 (over x, y, core).
Axes of the slice: x: 4, y: 8, z: 8, core: 2. Of those that a mesh axis runs over, the one named last changes fastest.
Arguments:
- head_queries: bfloat16 [8, 8192, 3072], P('dp', 'seq')
- head_keys: bfloat16 [8, 8192, 3072], P('dp', 'seq')
- head_values: bfloat16 [8, 8192, 3072], P('dp', 'seq'), may hold values from -6 to 6
- output_gradient: bfloat16 [8, 8192, 3072], P('dp', 'seq'), may hold values from -256 to 256
- key_adapter_input: bfloat16 [8, 8192, 64], P('dp', 'seq'), may hold values from -0.0234375 to 0.0234375
- value_adapter_input: bfloat16 [8, 8192, 64], P('dp', 'seq'), may hold values from -0.0234375 to 0.0234375
- key_block_lists: int32 [24, 64, 5], replicated, may hold values from 0 to 63, as said below
- live_block_counts: int32 [24, 64], replicated, may hold values from 1 to 5, as said below
Outputs:
- key_gradient: bfloat16 [8, 8192, 3072], P('dp', 'seq')
- value_gradient: bfloat16 [8, 8192, 3072], P('dp', 'seq')
- key_adapter_gradient: float32 [3072, 64], P(('dp', 'seq'))
- value_adapter_gradient: float32 [3072, 64], P(('dp', 'seq'))
The draws below stay inside these ranges and needn't reach their ends.
Inputs may be any that keep to these rules, and one draw needn't show every extreme that they name: Entry 0 of key_block_lists[h, b] is b; the first live_block_counts[h, b] entries are distinct blocks within 2 of b; later entries equal b. live_block_counts[h, b] is the smaller of a count of head h and the number of blocks within 2 of b.
All inputs are finite; a program needn't handle non-finite values.
Results may differ from the reference program's by a relative error of at most 0.04.
Values may be sent and summed in bfloat16 or wider, within the bound.
A program may use at most 64 MiB of HBM per device.

```python
import jax
import jax.numpy as jnp
from jax import lax

HEAD_COUNT = 24
HEAD_WIDTH = 128
ADAPTER_RANK = 64
BLK = 128
REACH = 2
TILES = 5
CLIP_TOKENS = 8192
CLIP_COUNT = 8
TOTAL_TOKENS = 65536


def pattern_draw(base_key):
    nblocks = CLIP_TOKENS // BLK
    tile_count = 2 * REACH + 1
    per_head = jax.random.randint(jax.random.fold_in(base_key, 11), (HEAD_COUNT,), 2, tile_count + 1)
    widest = jax.random.randint(jax.random.fold_in(base_key, 12), (), 0, HEAD_COUNT)
    narrow = (widest + 1 + jax.random.randint(jax.random.fold_in(base_key, 13), (), 0, HEAD_COUNT - 1)) % HEAD_COUNT
    per_head = per_head.at[widest].set(tile_count).at[narrow].set(1)
    blocks = jnp.arange(nblocks, dtype=jnp.int32)
    offsets = jnp.arange(tile_count, dtype=jnp.int32) - REACH
    target = blocks[:, None] + offsets[None, :]
    inside = (target >= 0) & (target < nblocks)
    rolls = jax.random.randint(jax.random.fold_in(base_key, 14), (HEAD_COUNT, nblocks, tile_count), 0, 65536) * tile_count + offsets[None, None, :] + REACH
    rolls = jnp.where(offsets[None, None, :] == 0, -1, rolls)
    rolls = jnp.where(inside[None], rolls, rolls + 65536 * tile_count * 2)
    ranked = jnp.argsort(rolls, axis=-1, stable=True)
    chosen = jnp.take_along_axis(jnp.broadcast_to(target[None], (HEAD_COUNT, nblocks, tile_count)), ranked, axis=-1)
    available = jnp.sum(inside.astype(jnp.int32), axis=1)
    counts = jnp.minimum(per_head[:, None], available[None, :])
    in_use = jnp.arange(tile_count, dtype=jnp.int32)[None, None, :] < counts[:, :, None]
    entries = jnp.where(in_use, chosen, blocks[None, :, None])
    return (entries.astype(jnp.int32), counts.astype(jnp.int32))


def attention_draw(base_key):
    shape = (CLIP_COUNT, CLIP_TOKENS, HEAD_COUNT * HEAD_WIDTH)
    queries = jax.random.normal(jax.random.fold_in(base_key, 21), shape, jnp.float32)
    keyset = jax.random.normal(jax.random.fold_in(base_key, 22), shape, jnp.float32)
    return (queries, keyset)


def draw_head_queries(key, part):
    return attention_draw(key)[0].astype(jnp.bfloat16)


def draw_head_keys(key, part):
    return attention_draw(key)[1].astype(jnp.bfloat16)


def draw_key_block_lists(key, part):
    return pattern_draw(key)[0]


def draw_live_block_counts(key, part):
    return pattern_draw(key)[1]


def raised(values, stream_key, source, target, blocks, factor):
    owner, partner = [(jnp.arange(values.shape[position]) // (values.shape[position] // blocks)).reshape([-1 if axis == position else 1 for axis in range(values.ndim)]) for position in (source, target)]
    chosen = jax.random.permutation(stream_key, blocks)[partner]
    strong = (owner == chosen) | (owner == (partner + blocks // 2) % blocks)
    return jnp.where(strong, factor * values, values)


def shard_levels(own_key, shape, pieces, smallest, high):
    gain, own = 1.0, jax.random.fold_in(own_key, 6)
    for position, blocks in pieces:
        heights = jnp.exp(jax.random.uniform(jax.random.fold_in(own, position), (blocks,), jnp.float32, smallest / len(pieces), high / len(pieces)))
        gain = gain * jnp.repeat(heights, shape[position] // blocks).reshape([-1 if axis == position else 1 for axis in range(len(shape))])
    return gain


def scatter_about(key, shape, scale, bound, pieces=(), kind=jnp.bfloat16):
    values = jax.random.normal(key, shape, jnp.float32) * scale
    if len(pieces) > 0:
        values = shard_levels(key, shape, pieces, -0.22, 0.18) * values
    return jnp.clip(values, min=-bound, max=bound).astype(kind)


def gaussian_with(stream_key, shape, scale, limit, pieces, heavy, kind=jnp.bfloat16):
    result = scale * jax.random.normal(stream_key, shape, jnp.float32)
    if pieces:
        result = result * shard_levels(stream_key, shape, pieces, -0.22, 0.18)
    return jnp.clip(raised(result, jax.random.fold_in(stream_key, 3), *heavy), -limit, limit).astype(kind)


def setup_inputs(seed: int = 0) -> dict:
    keys = jax.random.split(jax.random.key(seed), 9)
    head_queries = draw_head_queries(jax.random.fold_in(keys[8], 71), 0)
    head_keys = draw_head_keys(jax.random.fold_in(keys[8], 71), 0)
    head_values = scatter_about(keys[2], (CLIP_COUNT, CLIP_TOKENS, HEAD_COUNT * HEAD_WIDTH), 1.0, 6.0, ((0, 8), (1, 64)))
    output_gradient = gaussian_with(keys[3], (CLIP_COUNT, CLIP_TOKENS, HEAD_COUNT * HEAD_WIDTH), 16.0, 256.0, ((0, 8), (1, 64)), (1, 2, 64, 4.0))
    key_adapter_input = scatter_about(keys[4], (CLIP_COUNT, CLIP_TOKENS, ADAPTER_RANK), (TOTAL_TOKENS ** -0.5), 0.0234375, ((0, 8), (1, 64)))
    value_adapter_input = scatter_about(keys[5], (CLIP_COUNT, CLIP_TOKENS, ADAPTER_RANK), (TOTAL_TOKENS ** -0.5), 0.0234375, ((0, 8), (1, 64)))
    key_block_lists = draw_key_block_lists(jax.random.fold_in(keys[8], 71), 0)
    live_block_counts = draw_live_block_counts(jax.random.fold_in(keys[8], 71), 0)
    return {"head_queries": head_queries, "head_keys": head_keys, "head_values": head_values, "output_gradient": output_gradient, "key_adapter_input": key_adapter_input, "value_adapter_input": value_adapter_input, "key_block_lists": key_block_lists, "live_block_counts": live_block_counts}


def head_backward(query_tiles, key_tiles, value_tiles, grad_tiles, head_lists, head_counts):
    scaling = HEAD_WIDTH ** -0.5
    block_total = query_tiles.shape[0]
    picked_keys = jnp.take(key_tiles, head_lists, axis=0).astype(jnp.float32)
    picked_values = jnp.take(value_tiles, head_lists, axis=0).astype(jnp.float32)
    query_float = query_tiles.astype(jnp.float32)
    grad_float = grad_tiles.astype(jnp.float32)
    scores = jnp.einsum('bxd,btyd->btxy', query_float, picked_keys) * scaling
    in_use = (jnp.arange(TILES, dtype=jnp.int32)[None, :] < head_counts[:, None])[:, :, None, None]
    row_max = jnp.max(jnp.where(in_use, scores, -jnp.inf), axis=(1, 3), keepdims=True)
    exponent = jnp.where(in_use, jnp.exp(scores - row_max), 0.0)
    soft_probs = exponent / jnp.sum(exponent, axis=(1, 3), keepdims=True)
    soft_rounded = soft_probs.astype(jnp.bfloat16)
    dprobs = jnp.einsum('bxd,btyd->btxy', grad_float, picked_values)
    row_delta = jnp.sum(soft_rounded.astype(jnp.float32) * dprobs, axis=(1, 3), keepdims=True)
    score_grad = (soft_probs * (dprobs - row_delta)).astype(jnp.bfloat16)
    value_add = jnp.einsum('btxy,bxd->btyd', soft_rounded.astype(jnp.float32), grad_float)
    key_add = jnp.einsum('btxy,bxd->btyd', score_grad.astype(jnp.float32), query_float) * scaling
    value_acc = jnp.zeros((block_total, BLK, HEAD_WIDTH), jnp.float32).at[head_lists].add(value_add)
    key_acc = jnp.zeros((block_total, BLK, HEAD_WIDTH), jnp.float32).at[head_lists].add(key_add)
    return key_acc.astype(jnp.bfloat16), value_acc.astype(jnp.bfloat16)


def reference(head_queries, head_keys, head_values, output_gradient, key_adapter_input, value_adapter_input, key_block_lists, live_block_counts):
    nblocks = CLIP_TOKENS // BLK

    def arrange(array):
        return array.reshape(CLIP_COUNT, nblocks, BLK, HEAD_COUNT, HEAD_WIDTH).transpose(0, 3, 1, 2, 4).reshape(CLIP_COUNT * HEAD_COUNT, nblocks, BLK, HEAD_WIDTH)

    queries = arrange(head_queries)
    keyset = arrange(head_keys)
    valueset = arrange(head_values)
    gradset = arrange(output_gradient)

    def one_pair(pair_index):
        head_id = pair_index % HEAD_COUNT
        return head_backward(queries[pair_index], keyset[pair_index], valueset[pair_index], gradset[pair_index], key_block_lists[head_id], live_block_counts[head_id])

    key_parts, value_parts = lax.map(one_pair, jnp.arange(CLIP_COUNT * HEAD_COUNT, dtype=jnp.int32))

    def restore(array):
        return array.reshape(CLIP_COUNT, HEAD_COUNT, nblocks, BLK, HEAD_WIDTH).transpose(0, 2, 3, 1, 4).reshape(CLIP_COUNT, CLIP_TOKENS, HEAD_COUNT * HEAD_WIDTH)

    key_gradient = restore(key_parts)
    value_gradient = restore(value_parts)
    contract_dims = (((0,), (0,)), ((), ()))
    key_adapter_gradient = lax.dot_general(key_gradient.reshape(CLIP_COUNT * CLIP_TOKENS, HEAD_COUNT * HEAD_WIDTH), key_adapter_input.reshape(CLIP_COUNT * CLIP_TOKENS, ADAPTER_RANK), contract_dims, preferred_element_type=jnp.float32)
    value_adapter_gradient = lax.dot_general(value_gradient.reshape(CLIP_COUNT * CLIP_TOKENS, HEAD_COUNT * HEAD_WIDTH), value_adapter_input.reshape(CLIP_COUNT * CLIP_TOKENS, ADAPTER_RANK), contract_dims, preferred_element_type=jnp.float32)
    return key_gradient, value_gradient, key_adapter_gradient, value_adapter_gradient
```

```python
import functools

import jax
import jax.numpy as jnp
from jax import lax
from jax.experimental import pallas as pl
from jax.experimental.pallas import tpu as pltpu
from jax.sharding import PartitionSpec as P

HEAD_WIDTH = 128
BLK = 128
REACH = 2
WINDOW = 2 * REACH + 1
ROW_GROUP = 16
HUGE = 3.0e38
MESH = pl.DeviceIdType.MESH
F32 = jnp.float32
BF16 = jnp.bfloat16
NT = (((1,), (1,)), ((), ()))
NN = (((1,), (0,)), ((), ()))
TN = (((0,), (0,)), ((), ()))
OTHERS = (0, 1, 3, 4)


def kernel(
    planes, ring, heads, group,
    q, k, v, g, ka, va, bias,
    dk, dv, ad,
    hq, hg, es, ds, st, rs, fo, fr, zs, zr, own, xr, rows, ub, yr,
    h_send, h_recv, s_send, s_recv, f_send, f_recv, z_send, z_recv, x_send, x_recv, y_send, y_recv,
):
    scaling = HEAD_WIDTH ** (-0.5)
    z = lax.axis_index("dp")
    pos = lax.axis_index("seq")
    parity = lax.rem(pos, 2)
    partner = pos + 1 - 2 * parity
    width = heads * HEAD_WIDTH
    x_count = ring // group
    x_at = pos // group
    y_at = lax.rem(pos, group)
    x_rows = width // x_count
    y_rows = x_rows // group

    def peer(step):
        return lax.rem(pos + step + ring, ring)

    def x_peer(step):
        return lax.rem(x_at + step, x_count) * group + y_at

    def y_peer(step):
        return x_at * group + lax.rem(y_at + step, group)

    def z_peer(step):
        return lax.rem(z + step, planes)

    def piece(step):
        return lax.rem(z + 1 + step, planes)

    def remote(src, dst, send, recv, device):
        return pltpu.make_async_remote_copy(
            src_ref=src, dst_ref=dst, send_sem=send, recv_sem=recv,
            device_id=device, device_id_type=MESH,
        )

    def halo(flow, i, a, landing=False):
        source, store = (q, g)[a], (hq, hg)[a]
        cols = pl.ds(pl.multiple_of(piece(i) * width, 128), width)
        if flow == 0:
            src, slot, to = source.at[:, cols], 0, peer(2)
        elif flow == 1:
            src, slot, to = source.at[:, cols], 4, peer(-2)
        elif flow == 2:
            src, to = source.at[:, cols], partner
            slot = 3 - 2 * parity if landing else 1 + 2 * parity
        else:
            src, to = store.at[i, 4 - 4 * parity], partner
            slot = 1 + 2 * parity if landing else 3 - 2 * parity
        return remote(
            src, store.at[i, slot], h_send.at[flow, i, a], h_recv.at[flow, i, a], (z, to)
        )

    def stat_copy(j, i):
        return remote(st.at[j, i], rs.at[j, i], s_send.at[j, i], s_recv.at[j, i], (z, peer(j - 2)))

    def final_copy(j, i):
        return remote(fo.at[j, i], fr.at[j, i], f_send.at[j, i], f_recv.at[j, i], (z, peer(2 - j)))

    def z_copy(i):
        return remote(zs.at[i], zr.at[i], z_send.at[i], z_recv.at[i], (piece(i), pos))

    def x_copy(d):
        there = lax.rem(x_at + d, x_count)
        src = own.at[pl.ds(pl.multiple_of(there * x_rows, 8), x_rows)]
        return remote(src, xr.at[d - 1], x_send.at[d - 1], x_recv.at[d - 1], (z, x_peer(d)))

    def y_copy(d):
        there = lax.rem(y_at + d, group)
        return remote(
            ub.at[there], yr.at[d - 1], y_send.at[d - 1], y_recv.at[d - 1], (z, y_peer(d))
        )

    barrier = pltpu.get_barrier_semaphore()
    greeted = 0
    for d in (-2, -1, 1, 2):
        pl.semaphore_signal(barrier, inc=1, device_id=(z, peer(d)), device_id_type=MESH)
        greeted += 1
    for d in range(1, planes):
        pl.semaphore_signal(barrier, inc=1, device_id=(z_peer(d), pos), device_id_type=MESH)
        greeted += 1
    for d in range(1, x_count):
        pl.semaphore_signal(barrier, inc=1, device_id=(z, x_peer(d)), device_id_type=MESH)
        greeted += 1
    for d in range(1, group):
        pl.semaphore_signal(barrier, inc=1, device_id=(z, y_peer(d)), device_id_type=MESH)
        greeted += 1
    pl.semaphore_wait(barrier, greeted)

    @pl.loop(0, planes)
    def _(i):
        for flow in (0, 1, 2):
            for a in (0, 1):
                halo(flow, i, a).start()

    def head_cols(i, h):
        return pl.ds(pl.multiple_of(piece(i) * width + h * HEAD_WIDTH, 128), HEAD_WIDTH)

    def operand(own_ref, store, i, h, j):
        if isinstance(j, int) and j == 2:
            return own_ref[:, head_cols(i, h)]
        return store[i, j, :, h * HEAD_WIDTH : (h + 1) * HEAD_WIDTH]

    def tile_stats(i, h, j):
        held = lax.rem(i, 3)
        scores = scaling * lax.dot_general(
            k[:, head_cols(i, h)], operand(q, hq, i, h, j), NT, preferred_element_type=F32
        )
        dprobs = lax.dot_general(
            v[:, head_cols(i, h)], operand(g, hg, i, h, j), NT, preferred_element_type=F32
        )
        top = jnp.max(scores, axis=0, keepdims=True)
        grown = jnp.exp(scores - top)
        es[held, h, j] = grown
        ds[held, h, j] = dprobs
        st[j, i, 0, h : h + 1, :] = top
        st[j, i, 1, h : h + 1, :] = jnp.sum(grown, axis=0, keepdims=True)
        st[j, i, 2, h : h + 1, :] = jnp.sum(grown * dprobs, axis=0, keepdims=True)

    def first_pass(i):
        for flow in (0, 1):
            for a in (0, 1):
                halo(flow, i, a, True).wait_recv()
        for a in (0, 1):
            halo(3, i, a).start()
        for a in (0, 1):
            halo(2, i, a, True).wait_recv()
        for h in range(heads):
            for j in (2, 0, 4, 3 - 2 * parity):
                tile_stats(i, h, j)
        for a in (0, 1):
            halo(3, i, a, True).wait_recv()
        for h in range(heads):
            tile_stats(i, h, 1 + 2 * parity)
        for j in OTHERS:
            stat_copy(j, i).start()

    def combine(i):
        for j in OTHERS:
            stat_copy(j, i).wait_recv()
        tops, totals, sums, shut = [], [], [], []
        for j in range(WINDOW):
            part = st if j == 2 else rs
            closed = bias[j, piece(i)]
            shut.append(closed)
            tops.append(part[j, i, 0, 0:heads, :] + closed)
            totals.append(part[j, i, 1, 0:heads, :])
            sums.append(part[j, i, 2, 0:heads, :])
        top = functools.reduce(jnp.maximum, tops)
        weights = [jnp.exp(t - top) for t in tops]
        total = sum(w * t for w, t in zip(weights, totals))
        delta = sum(w * t for w, t in zip(weights, sums)) / total
        level = top + jnp.log(total)
        for j in range(WINDOW):
            fo[j, i, 0, 0:heads, :] = jnp.where(shut[j] < 0, HUGE, level)
            fo[j, i, 1, 0:heads, :] = delta
        for j in OTHERS:
            final_copy(j, i).start()

    def second_pass(i):
        held = lax.rem(i, 3)
        for j in OTHERS:
            final_copy(j, i).wait_recv()
        for h in range(heads):
            key_sum = jnp.zeros((BLK, HEAD_WIDTH), F32)
            value_sum = jnp.zeros((BLK, HEAD_WIDTH), F32)
            for j in range(WINDOW):
                final = fo if j == 2 else fr
                factor = jnp.exp(st[j, i, 0, h : h + 1, :] - final[j, i, 0, h : h + 1, :])
                probs = es[held, h, j] * factor
                score_grad = (probs * (ds[held, h, j] - final[j, i, 1, h : h + 1, :])).astype(BF16)
                value_sum += lax.dot_general(
                    probs.astype(BF16), operand(g, hg, i, h, j), NN, preferred_element_type=F32
                )
                key_sum += lax.dot_general(
                    score_grad, operand(q, hq, i, h, j), NN, preferred_element_type=F32
                )
            key_out = (key_sum * scaling).astype(BF16)
            value_out = value_sum.astype(BF16)
            dk[:, head_cols(i, h)] = key_out
            dv[:, head_cols(i, h)] = value_out
            term = lax.dot_general(key_out, ka[...], TN, preferred_element_type=F32)
            term += lax.dot_general(value_out, va[...], TN, preferred_element_type=F32)
            own[h * HEAD_WIDTH : (h + 1) * HEAD_WIDTH, :] = term

        @pl.when(i < planes - 1)
        def _():
            zs[i] = own[...].astype(BF16)
            z_copy(i).start()

    @pl.loop(0, planes + 2)
    def _(t):
        @pl.when(t < planes)
        def _():
            first_pass(t)

        @pl.when((t >= 1) & (t < planes + 1))
        def _():
            combine(t - 1)

        @pl.when(t >= 2)
        def _():
            second_pass(t - 2)

    total = own[...]
    for i in range(planes - 1):
        z_copy(i).wait_recv()
        total += zr[i].astype(F32)
    own[...] = total
    for d in range(1, x_count):
        x_copy(d).start()
    mine = own[pl.ds(pl.multiple_of(x_at * x_rows, 8), x_rows), :]
    for d in range(1, x_count):
        x_copy(d).wait_recv()
        mine += xr[d - 1]
    rows[...] = mine
    ub[...] = jnp.zeros_like(ub)
    for n in range(group):
        ub[n, 0:y_rows, :] = rows[n * y_rows : (n + 1) * y_rows, :]
    for d in range(1, group):
        y_copy(d).start()
    last = ub[y_at]
    for d in range(1, group):
        y_copy(d).wait_recv()
        last += yr[d - 1]
    ad[...] = last

    @pl.loop(0, planes)
    def _(i):
        for flow in range(4):
            for a in (0, 1):
                halo(flow, i, a).wait_send()
        for j in OTHERS:
            stat_copy(j, i).wait_send()
            final_copy(j, i).wait_send()

    for i in range(planes - 1):
        z_copy(i).wait_send()
    for d in range(1, x_count):
        x_copy(d).wait_send()
    for d in range(1, group):
        y_copy(d).wait_send()


def body(planes, ring, group, hq, hk, hv, og, ka, va, lists, counts):
    head_count = lists.shape[0]
    heads = head_count // planes
    width = heads * HEAD_WIDTH
    rank = ka.shape[-1]
    x_count = ring // group
    x_rows = width // x_count
    y_rows = x_rows // group
    y_pad = -(-y_rows // 8) * 8
    block = lax.axis_index("seq")
    own_lists = lax.dynamic_index_in_dim(lists, block, 1, keepdims=False)
    own_counts = lax.dynamic_index_in_dim(counts, block, 1, keepdims=False)
    used = jnp.arange(lists.shape[2])[None, :] < own_counts[:, None]
    holders = block + REACH - jnp.arange(WINDOW)
    live = jnp.any((own_lists[None] == holders[:, None, None]) & used[None], axis=2)
    bias = jnp.where(live, 0.0, -jnp.inf).astype(F32).reshape(WINDOW, planes, heads, 1)
    bias = jnp.broadcast_to(bias, (WINDOW, planes, heads, BLK))
    ka_wide = jnp.pad(ka[0], ((0, 0), (0, rank)))
    va_wide = jnp.pad(va[0], ((0, 0), (rank, 0)))
    tokens, columns = hq.shape[1:]
    sems = pltpu.SemaphoreType.DMA
    dk, dv, ad = pl.pallas_call(
        functools.partial(kernel, planes, ring, heads, group),
        out_shape=(
            jax.ShapeDtypeStruct((tokens, columns), BF16),
            jax.ShapeDtypeStruct((tokens, columns), BF16),
            jax.ShapeDtypeStruct((y_pad, 2 * rank), F32),
        ),
        in_specs=[pl.BlockSpec(memory_space=pltpu.VMEM)] * 7,
        out_specs=[pl.BlockSpec(memory_space=pltpu.VMEM)] * 3,
        scratch_shapes=[
            pltpu.VMEM((planes, WINDOW, BLK, width), BF16),
            pltpu.VMEM((planes, WINDOW, BLK, width), BF16),
            pltpu.VMEM((3, heads, WINDOW, BLK, BLK), F32),
            pltpu.VMEM((3, heads, WINDOW, BLK, BLK), F32),
            pltpu.VMEM((WINDOW, planes, 3, 8, BLK), F32),
            pltpu.VMEM((WINDOW, planes, 3, 8, BLK), F32),
            pltpu.VMEM((WINDOW, planes, 2, 8, BLK), F32),
            pltpu.VMEM((WINDOW, planes, 2, 8, BLK), F32),
            pltpu.VMEM((max(planes - 1, 1), width, 2 * rank), BF16),
            pltpu.VMEM((max(planes - 1, 1), width, 2 * rank), BF16),
            pltpu.VMEM((width, 2 * rank), F32),
            pltpu.VMEM((max(x_count - 1, 1), x_rows, 2 * rank), F32),
            pltpu.VMEM((x_rows, 2 * rank), F32),
            pltpu.VMEM((group, y_pad, 2 * rank), F32),
            pltpu.VMEM((group - 1, y_pad, 2 * rank), F32),
            sems((4, planes, 2)),
            sems((4, planes, 2)),
            sems((WINDOW, planes)),
            sems((WINDOW, planes)),
            sems((WINDOW, planes)),
            sems((WINDOW, planes)),
            sems((max(planes - 1, 1),)),
            sems((max(planes - 1, 1),)),
            sems((max(x_count - 1, 1),)),
            sems((max(x_count - 1, 1),)),
            sems((group - 1,)),
            sems((group - 1,)),
        ],
        compiler_params=pltpu.CompilerParams(
            collective_id=0, has_side_effects=True, vmem_limit_bytes=60 * 1024 * 1024
        ),
    )(hq[0], hk[0], hv[0], og[0], ka_wide, va_wide, bias)
    return dk[None], dv[None], ad[:y_rows, :rank], ad[:y_rows, rank:]


def solution(mesh, group=ROW_GROUP):
    split = P("dp", "seq", None)
    rows = P(("dp", "seq"), None)
    return jax.shard_map(
        functools.partial(body, mesh.shape["dp"], mesh.shape["seq"], group),
        mesh=mesh,
        in_specs=(split,) * 6 + (P(), P()),
        out_specs=(split, split, rows, rows),
        check_vma=False,
    )
```

```python
import functools

import jax
import jax.numpy as jnp
from jax import lax
from jax.experimental import pallas as pl
from jax.experimental.pallas import tpu as pltpu
from jax.sharding import PartitionSpec as P

HEAD_WIDTH = 128
BLK = 128
REACH = 2
WINDOW = 2 * REACH + 1
ROW_GROUP = 16
AHEAD = 2
LAG_STATS = 2
LAG_LAST = 4
HUGE = 3.0e38
MESH = pl.DeviceIdType.MESH
F32 = jnp.float32
BF16 = jnp.bfloat16
NT = (((1,), (1,)), ((), ()))
NN = (((1,), (0,)), ((), ()))
TN = (((0,), (0,)), ((), ()))
OTHERS = (0, 1, 3, 4)


def kernel(
    planes, ring, heads, group,
    q_hbm, k_hbm, v_hbm, g_hbm, ka, va, lists, counts,
    dk_hbm, dv_hbm, ad,
    q, k, v, g, dk, dv, wide, shut, hq, hg, es, ds, st, rs, fo, fr, zs, zr, own, xr, rows, ub, yr,
    in_sem, out_sem, h_send, h_recv, s_send, s_recv, f_send, f_recv, z_send, z_recv, x_send, x_recv, y_send, y_recv,
):
    scaling = HEAD_WIDTH ** (-0.5)
    z = lax.axis_index("dp")
    pos = lax.axis_index("seq")
    parity = lax.rem(pos, 2)
    partner = pos + 1 - 2 * parity
    width = heads * HEAD_WIDTH
    x_count = ring // group
    x_at = pos // group
    y_at = lax.rem(pos, group)
    x_rows = width // x_count
    y_rows = x_rows // group

    def peer(step):
        return lax.rem(pos + step + ring, ring)

    def x_peer(step):
        return lax.rem(x_at + step, x_count) * group + y_at

    def y_peer(step):
        return x_at * group + lax.rem(y_at + step, group)

    def z_peer(step):
        return lax.rem(z + step, planes)

    def piece(step):
        odd = lax.rem(step, 2)
        far = (step + odd) // 2
        return lax.rem(z + planes // 2 + (2 * odd - 1) * far + planes, planes)

    def remote(src, dst, send, recv, device):
        return pltpu.make_async_remote_copy(
            src_ref=src, dst_ref=dst, send_sem=send, recv_sem=recv,
            device_id=device, device_id_type=MESH,
        )

    def halo(flow, i, a, landing=False):
        source, store = (q_hbm, g_hbm)[a], (hq, hg)[a]
        cols = pl.ds(pl.multiple_of(piece(i) * width, 128), width)
        if flow == 0:
            src, slot, to = source.at[:, cols], 0, peer(2)
        elif flow == 1:
            src, slot, to = source.at[:, cols], 4, peer(-2)
        elif flow == 2:
            src, to = source.at[:, cols], partner
            slot = 3 - 2 * parity if landing else 1 + 2 * parity
        else:
            src, to = store.at[i, 4 - 4 * parity], partner
            slot = 1 + 2 * parity if landing else 3 - 2 * parity
        return remote(
            src, store.at[i, slot], h_send.at[flow, i, a], h_recv.at[flow, i, a], (z, to)
        )

    def stat_copy(j, i):
        return remote(st.at[j, i], rs.at[j, i], s_send.at[j, i], s_recv.at[j, i], (z, peer(j - 2)))

    def final_copy(j, i):
        return remote(fo.at[j, i], fr.at[j, i], f_send.at[j, i], f_recv.at[j, i], (z, peer(2 - j)))

    def z_copy(i):
        onward = lax.rem(z + 1 - 2 * lax.rem(i, 2) + planes, planes)
        return remote(zs.at[i], zr.at[i], z_send.at[i], z_recv.at[i], (onward, pos))

    def x_copy(d):
        there = lax.rem(x_at + d, x_count)
        src = own.at[pl.ds(pl.multiple_of(there * x_rows, 8), x_rows)]
        return remote(src, xr.at[d - 1], x_send.at[d - 1], x_recv.at[d - 1], (z, x_peer(d)))

    def y_copy(d):
        there = lax.rem(y_at + d, group)
        return remote(
            ub.at[there], yr.at[d - 1], y_send.at[d - 1], y_recv.at[d - 1], (z, y_peer(d))
        )

    def out_copy(i, a):
        cols = pl.ds(pl.multiple_of(piece(i) * width, 128), width)
        src, dst = ((dk, dk_hbm), (dv, dv_hbm))[a]
        return pltpu.make_async_copy(src.at[:, cols], dst.at[:, cols], out_sem.at[i, a])

    loads = [
        pltpu.make_async_copy(src, dst, in_sem.at[n])
        for n, (src, dst) in enumerate(((q_hbm, q), (k_hbm, k), (g_hbm, g), (v_hbm, v)))
    ]
    for load in loads:
        load.start()
    wide[...] = jnp.concatenate([ka[...], va[...]], axis=0).astype(F32).T.astype(BF16)
    lane = lax.broadcasted_iota(jnp.int32, counts.shape, 1)
    for j in range(WINDOW):
        hits = [
            (lists[n] == lane + (REACH - j)) & (counts[...] > n) & (lane == pos)
            for n in range(lists.shape[0])
        ]
        found = sum(jnp.where(hit, 1.0, 0.0) for hit in hits)
        column = jnp.sum(found, axis=1, keepdims=True)
        shut[j] = jnp.broadcast_to(jnp.where(column > 0.5, 0.0, -jnp.inf), shut.shape[1:])

    barrier = pltpu.get_barrier_semaphore()
    greeted = 0
    for d in (-2, -1, 1, 2):
        pl.semaphore_signal(barrier, inc=1, device_id=(z, peer(d)), device_id_type=MESH)
        greeted += 1
    for d in (1, planes - 1):
        pl.semaphore_signal(barrier, inc=1, device_id=(z_peer(d), pos), device_id_type=MESH)
        greeted += 1
    for d in range(1, x_count):
        pl.semaphore_signal(barrier, inc=1, device_id=(z, x_peer(d)), device_id_type=MESH)
        greeted += 1
    for d in range(1, group):
        pl.semaphore_signal(barrier, inc=1, device_id=(z, y_peer(d)), device_id_type=MESH)
        greeted += 1
    pl.semaphore_wait(barrier, greeted)

    def send_halo(i):
        for a in (0, 1):
            for flow in (0, 1, 2):
                halo(flow, i, a).start()

    for i in range(min(AHEAD, planes)):
        send_halo(i)
    for load in loads:
        load.wait()

    def head_cols(i, h):
        return pl.ds(pl.multiple_of(piece(i) * width + h * HEAD_WIDTH, 128), HEAD_WIDTH)

    def operand(own_ref, store, i, h, j):
        if isinstance(j, int) and j == 2:
            return own_ref[:, head_cols(i, h)]
        return store[i, j, :, h * HEAD_WIDTH : (h + 1) * HEAD_WIDTH]

    def tile_stats(i, h, j):
        held = lax.rem(i, LAG_LAST + 1)
        scores = scaling * lax.dot_general(
            k[:, head_cols(i, h)], operand(q, hq, i, h, j), NT, preferred_element_type=F32
        )
        dprobs = lax.dot_general(
            v[:, head_cols(i, h)], operand(g, hg, i, h, j), NT, preferred_element_type=F32
        )
        top = jnp.max(scores, axis=0, keepdims=True)
        grown = jnp.exp(scores - top)
        es[held, h, j] = grown
        ds[held, h, j] = dprobs
        st[j, i, 0, h : h + 1, :] = top
        st[j, i, 1, h : h + 1, :] = jnp.sum(grown, axis=0, keepdims=True)
        st[j, i, 2, h : h + 1, :] = jnp.sum(grown * dprobs, axis=0, keepdims=True)

    def arrive(i):
        for a in (0, 1):
            for flow in (0, 1):
                halo(flow, i, a, True).wait_recv()
            halo(3, i, a).start()

    def first_tiles(i):
        for a in (0, 1):
            halo(2, i, a, True).wait_recv()
        for h in range(heads):
            for j in (2, 0, 4, 3 - 2 * parity):
                tile_stats(i, h, j)

    def last_tiles(i):
        for a in (0, 1):
            halo(3, i, a, True).wait_recv()
        for h in range(heads):
            tile_stats(i, h, 1 + 2 * parity)
        for j in OTHERS:
            stat_copy(j, i).start()

    def combine(i):
        for j in OTHERS:
            stat_copy(j, i).wait_recv()
        tops, totals, sums, dead = [], [], [], []
        for j in range(WINDOW):
            part = st if j == 2 else rs
            closed = jnp.concatenate(
                [shut[j, pl.ds(piece(i) * heads + h, 1), :] for h in range(heads)], axis=0
            )
            dead.append(closed < 0)
            tops.append(part[j, i, 0, 0:heads, :] + closed)
            totals.append(part[j, i, 1, 0:heads, :])
            sums.append(part[j, i, 2, 0:heads, :])
        top = functools.reduce(jnp.maximum, tops)
        weights = [jnp.exp(t - top) for t in tops]
        total = sum(w * t for w, t in zip(weights, totals))
        delta = sum(w * t for w, t in zip(weights, sums)) / total
        level = top + jnp.log(total)
        for j in range(WINDOW):
            fo[j, i, 0, 0:heads, :] = jnp.where(dead[j], HUGE, level)
            fo[j, i, 1, 0:heads, :] = delta
        for j in OTHERS:
            final_copy(j, i).start()

    def second_pass(i):
        held = lax.rem(i, LAG_LAST + 1)
        for j in OTHERS:
            final_copy(j, i).wait_recv()
        for h in range(heads):
            key_sum = jnp.zeros((BLK, HEAD_WIDTH), F32)
            value_sum = jnp.zeros((BLK, HEAD_WIDTH), F32)
            for j in range(WINDOW):
                final = fo if j == 2 else fr
                factor = jnp.exp(st[j, i, 0, h : h + 1, :] - final[j, i, 0, h : h + 1, :])
                probs = es[held, h, j] * factor
                score_grad = (probs * (ds[held, h, j] - final[j, i, 1, h : h + 1, :])).astype(BF16)
                value_sum += lax.dot_general(
                    probs.astype(BF16), operand(g, hg, i, h, j), NN, preferred_element_type=F32
                )
                key_sum += lax.dot_general(
                    score_grad, operand(q, hq, i, h, j), NN, preferred_element_type=F32
                )
            key_out = (key_sum * scaling).astype(BF16)
            value_out = value_sum.astype(BF16)
            dk[:, head_cols(i, h)] = key_out
            dv[:, head_cols(i, h)] = value_out
            key_term = lax.dot_general(key_out, wide[...], TN, preferred_element_type=F32)
            value_term = lax.dot_general(value_out, wide[...], TN, preferred_element_type=F32)
            side = lax.broadcasted_iota(jnp.int32, key_term.shape, 1)
            term = jnp.where(side < ka.shape[0], key_term, value_term)
            own[h * HEAD_WIDTH : (h + 1) * HEAD_WIDTH, :] = term
        for a in (0, 1):
            out_copy(i, a).start()

        @pl.when(i >= 2)
        def _():
            z_copy(i - 2).wait_recv()
            own[...] += zr[i - 2].astype(F32)

        @pl.when(i < planes - 1)
        def _():
            zs[i] = own[...].astype(BF16)
            z_copy(i).start()

    @pl.loop(0, planes + LAG_LAST)
    def _(t):
        @pl.when(t < planes)
        def _():
            arrive(t)

        @pl.when(t < planes - AHEAD)
        def _():
            send_halo(t + AHEAD)

        @pl.when(t < planes)
        def _():
            first_tiles(t)

        @pl.when((t >= LAG_STATS) & (t < planes + LAG_STATS))
        def _():
            combine(t - LAG_STATS)

        @pl.when(t < planes)
        def _():
            last_tiles(t)

        @pl.when(t >= LAG_LAST)
        def _():
            second_pass(t - LAG_LAST)

    z_copy(planes - 2).wait_recv()
    own[...] += zr[planes - 2].astype(F32)
    for d in range(1, x_count):
        x_copy(d).start()
    mine = own[pl.ds(pl.multiple_of(x_at * x_rows, 8), x_rows), :]
    for d in range(1, x_count):
        x_copy(d).wait_recv()
        mine += xr[d - 1]
    rows[...] = mine
    ub[...] = jnp.zeros_like(ub)
    for n in range(group):
        ub[n, 0:y_rows, :] = rows[n * y_rows : (n + 1) * y_rows, :]
    for d in range(1, group):
        y_copy(d).start()
    last = ub[y_at]
    for d in range(1, group):
        y_copy(d).wait_recv()
        last += yr[d - 1]
    ad[...] = last

    @pl.loop(0, planes)
    def _(i):
        for flow in range(4):
            for a in (0, 1):
                halo(flow, i, a).wait_send()
        for a in (0, 1):
            out_copy(i, a).wait()
        for j in OTHERS:
            stat_copy(j, i).wait_send()
            final_copy(j, i).wait_send()

    for i in range(planes - 1):
        z_copy(i).wait_send()
    for d in range(1, x_count):
        x_copy(d).wait_send()
    for d in range(1, group):
        y_copy(d).wait_send()


def finish(parts, part, dk, dv, ad, dk_out, dv_out, ka_grad, va_grad, hold, in_sem, out_sem):
    ins, outs = [], []
    for n in range(parts):
        cols = pl.ds(n * part, part)
        for a, (src, dst) in enumerate(((dk, dk_out), (dv, dv_out))):
            ins.append(pltpu.make_async_copy(src.at[:, cols], hold.at[a, n], in_sem.at[a, n]))
            outs.append(pltpu.make_async_copy(hold.at[a, n], dst.at[:, cols], out_sem.at[a, n]))
    for load in ins:
        load.start()
    rank = ka_grad.shape[1]
    ka_grad[...] = ad[0 : ka_grad.shape[0], 0:rank]
    va_grad[...] = ad[0 : ka_grad.shape[0], rank:]
    for load, store in zip(ins, outs):
        load.wait()
        store.start()
    for store in outs:
        store.wait()


def body(planes, ring, group, hq, hk, hv, og, ka, va, lists, counts):
    head_count = lists.shape[0]
    heads = head_count // planes
    width = heads * HEAD_WIDTH
    rank = ka.shape[-1]
    x_count = ring // group
    x_rows = width // x_count
    y_rows = x_rows // group
    y_pad = -(-y_rows // 8) * 8
    tokens, columns = hq.shape[1:]
    sems = pltpu.SemaphoreType.DMA
    dk, dv, ad = pl.pallas_call(
        functools.partial(kernel, planes, ring, heads, group),
        out_shape=(
            jax.ShapeDtypeStruct((tokens, columns), BF16),
            jax.ShapeDtypeStruct((tokens, columns), BF16),
            jax.ShapeDtypeStruct((y_pad, 2 * rank), F32),
        ),
        in_specs=[pl.BlockSpec(memory_space=pl.ANY)] * 4
        + [pl.BlockSpec(memory_space=pltpu.VMEM)] * 4,
        out_specs=[pl.BlockSpec(memory_space=pl.ANY)] * 2
        + [pl.BlockSpec(memory_space=pltpu.VMEM)],
        scratch_shapes=[
            *[pltpu.VMEM((tokens, columns), BF16)] * 6,
            pltpu.VMEM((tokens, 2 * rank), BF16),
            pltpu.VMEM((WINDOW, head_count, BLK), F32),
            pltpu.VMEM((planes, WINDOW, BLK, width), BF16),
            pltpu.VMEM((planes, WINDOW, BLK, width), BF16),
            pltpu.VMEM((LAG_LAST + 1, heads, WINDOW, BLK, BLK), F32),
            pltpu.VMEM((LAG_LAST + 1, heads, WINDOW, BLK, BLK), F32),
            pltpu.VMEM((WINDOW, planes, 3, 8, BLK), F32),
            pltpu.VMEM((WINDOW, planes, 3, 8, BLK), F32),
            pltpu.VMEM((WINDOW, planes, 2, 8, BLK), F32),
            pltpu.VMEM((WINDOW, planes, 2, 8, BLK), F32),
            pltpu.VMEM((max(planes - 1, 1), width, 2 * rank), BF16),
            pltpu.VMEM((max(planes - 1, 1), width, 2 * rank), BF16),
            pltpu.VMEM((width, 2 * rank), F32),
            pltpu.VMEM((max(x_count - 1, 1), x_rows, 2 * rank), F32),
            pltpu.VMEM((x_rows, 2 * rank), F32),
            pltpu.VMEM((group, y_pad, 2 * rank), F32),
            pltpu.VMEM((group - 1, y_pad, 2 * rank), F32),
            sems((4,)),
            sems((planes, 2)),
            sems((4, planes, 2)),
            sems((4, planes, 2)),
            sems((WINDOW, planes)),
            sems((WINDOW, planes)),
            sems((WINDOW, planes)),
            sems((WINDOW, planes)),
            sems((max(planes - 1, 1),)),
            sems((max(planes - 1, 1),)),
            sems((max(x_count - 1, 1),)),
            sems((max(x_count - 1, 1),)),
            sems((group - 1,)),
            sems((group - 1,)),
        ],
        compiler_params=pltpu.CompilerParams(
            collective_id=0, has_side_effects=True, vmem_limit_bytes=60 * 1024 * 1024
        ),
    )(hq[0], hk[0], hv[0], og[0], ka[0].T, va[0].T, lists.transpose(2, 0, 1), counts)
    parts = 4
    part = columns // parts
    dk, dv, ka_grad, va_grad = pl.pallas_call(
        functools.partial(finish, parts, part),
        out_shape=(
            jax.ShapeDtypeStruct((tokens, columns), BF16),
            jax.ShapeDtypeStruct((tokens, columns), BF16),
            jax.ShapeDtypeStruct((y_rows, rank), F32),
            jax.ShapeDtypeStruct((y_rows, rank), F32),
        ),
        in_specs=[pl.BlockSpec(memory_space=pl.ANY)] * 2
        + [pl.BlockSpec(memory_space=pltpu.VMEM)],
        out_specs=[pl.BlockSpec(memory_space=pl.ANY)] * 2
        + [pl.BlockSpec(memory_space=pltpu.VMEM)] * 2,
        scratch_shapes=[
            pltpu.VMEM((2, parts, tokens, part), BF16),
            sems((2, parts)),
            sems((2, parts)),
        ],
    )(dk, dv, ad)
    return dk[None], dv[None], ka_grad, va_grad


def solution(mesh, group=ROW_GROUP):
    split = P("dp", "seq", None)
    rows = P(("dp", "seq"), None)
    return jax.shard_map(
        functools.partial(body, mesh.shape["dp"], mesh.shape["seq"], group),
        mesh=mesh,
        in_specs=(split,) * 6 + (P(), P()),
        out_specs=(split, split, rows, rows),
        check_vma=False,
    )
```

```python
import functools

import jax
import jax.numpy as jnp
from jax import lax
from jax.experimental import pallas as pl
from jax.experimental.pallas import tpu as pltpu
from jax.sharding import PartitionSpec as P

HEAD_WIDTH = 128
BLK = 128
REACH = 2
WINDOW = 2 * REACH + 1
ROW_GROUP = 16
AHEAD = 2
LAG_STATS = 2
LAG_LAST = 4
HUGE = 3.0e38
MESH = pl.DeviceIdType.MESH
F32 = jnp.float32
BF16 = jnp.bfloat16
NT = (((1,), (1,)), ((), ()))
NN = (((1,), (0,)), ((), ()))
TN = (((0,), (0,)), ((), ()))
OTHERS = (0, 1, 3, 4)


def kernel(
    planes, ring, heads, group,
    q_hbm, k_hbm, v_hbm, g_hbm, ka, va, lists, counts,
    dk_hbm, dv_hbm, ad,
    q, k, v, g, dk, dv, wide, shut, hq, hg, es, ds, st, rs, fo, fr, zs, zr, own, own16, xr, rows, ub, yr,
    in_sem, out_sem, h_send, h_recv, s_send, s_recv, f_send, f_recv, z_send, z_recv, x_send, x_recv, y_send, y_recv,
):
    scaling = HEAD_WIDTH ** (-0.5)
    z = lax.axis_index("dp")
    pos = lax.axis_index("seq")
    parity = lax.rem(pos, 2)
    partner = pos + 1 - 2 * parity
    width = heads * HEAD_WIDTH
    x_count = ring // group
    x_at = pos // group
    y_at = lax.rem(pos, group)
    x_rows = width // x_count
    y_rows = x_rows // group

    def peer(step):
        return lax.rem(pos + step + ring, ring)

    def x_peer(step):
        return lax.rem(x_at + step, x_count) * group + y_at

    def y_peer(step):
        return x_at * group + lax.rem(y_at + step, group)

    def z_peer(step):
        return lax.rem(z + step, planes)

    def piece(step):
        odd = lax.rem(step, 2)
        far = (step + odd) // 2
        return lax.rem(z + planes // 2 + (2 * odd - 1) * far + planes, planes)

    def remote(src, dst, send, recv, device):
        return pltpu.make_async_remote_copy(
            src_ref=src, dst_ref=dst, send_sem=send, recv_sem=recv,
            device_id=device, device_id_type=MESH,
        )

    def halo(flow, i, a, landing=False):
        source, store = (q_hbm, g_hbm)[a], (hq, hg)[a]
        cols = pl.ds(pl.multiple_of(piece(i) * width, 128), width)
        if flow == 0:
            src, slot, to = source.at[:, cols], 0, peer(2)
        elif flow == 1:
            src, slot, to = source.at[:, cols], 4, peer(-2)
        elif flow == 2:
            src, to = source.at[:, cols], partner
            slot = 3 - 2 * parity if landing else 1 + 2 * parity
        else:
            src, to = store.at[i, 4 - 4 * parity], partner
            slot = 1 + 2 * parity if landing else 3 - 2 * parity
        return remote(
            src, store.at[i, slot], h_send.at[flow, i, a], h_recv.at[flow, i, a], (z, to)
        )

    def stat_copy(j, i):
        return remote(st.at[j, i], rs.at[j, i], s_send.at[j, i], s_recv.at[j, i], (z, peer(j - 2)))

    def final_copy(j, i):
        return remote(fo.at[j, i], fr.at[j, i], f_send.at[j, i], f_recv.at[j, i], (z, peer(2 - j)))

    def z_copy(i):
        onward = lax.rem(z + 1 - 2 * lax.rem(i, 2) + planes, planes)
        return remote(zs.at[i], zr.at[i], z_send.at[i], z_recv.at[i], (onward, pos))

    def x_copy(d):
        there = lax.rem(x_at + d, x_count)
        src = own16.at[pl.ds(pl.multiple_of(there * x_rows, 16), x_rows)]
        return remote(src, xr.at[d - 1], x_send.at[d - 1], x_recv.at[d - 1], (z, x_peer(d)))

    def y_copy(d):
        there = lax.rem(y_at + d, group)
        return remote(
            ub.at[there], yr.at[d - 1], y_send.at[d - 1], y_recv.at[d - 1], (z, y_peer(d))
        )

    def out_copy(i, a):
        cols = pl.ds(pl.multiple_of(piece(i) * width, 128), width)
        src, dst = ((dk, dk_hbm), (dv, dv_hbm))[a]
        return pltpu.make_async_copy(src.at[:, cols], dst.at[:, cols], out_sem.at[i, a])

    loads = [
        pltpu.make_async_copy(src, dst, in_sem.at[n])
        for n, (src, dst) in enumerate(((q_hbm, q), (k_hbm, k), (g_hbm, g), (v_hbm, v)))
    ]
    for load in loads:
        load.start()
    wide[...] = jnp.concatenate([ka[...], va[...]], axis=0).astype(F32).T.astype(BF16)
    lane = lax.broadcasted_iota(jnp.int32, counts.shape, 1)
    for j in range(WINDOW):
        hits = [
            (lists[n] == lane + (REACH - j)) & (counts[...] > n) & (lane == pos)
            for n in range(lists.shape[0])
        ]
        found = sum(jnp.where(hit, 1.0, 0.0) for hit in hits)
        column = jnp.sum(found, axis=1, keepdims=True)
        shut[j] = jnp.broadcast_to(jnp.where(column > 0.5, 0.0, -jnp.inf), shut.shape[1:])

    barrier = pltpu.get_barrier_semaphore()
    greeted = 0
    for d in (-2, -1, 1, 2):
        pl.semaphore_signal(barrier, inc=1, device_id=(z, peer(d)), device_id_type=MESH)
        greeted += 1
    for d in (1, planes - 1):
        pl.semaphore_signal(barrier, inc=1, device_id=(z_peer(d), pos), device_id_type=MESH)
        greeted += 1
    for d in range(1, x_count):
        pl.semaphore_signal(barrier, inc=1, device_id=(z, x_peer(d)), device_id_type=MESH)
        greeted += 1
    for d in range(1, group):
        pl.semaphore_signal(barrier, inc=1, device_id=(z, y_peer(d)), device_id_type=MESH)
        greeted += 1
    pl.semaphore_wait(barrier, greeted)

    def send_halo(i):
        for a in (0, 1):
            for flow in (0, 1, 2):
                halo(flow, i, a).start()

    for i in range(min(AHEAD, planes)):
        send_halo(i)
    for load in loads:
        load.wait()

    def head_cols(i, h):
        return pl.ds(pl.multiple_of(piece(i) * width + h * HEAD_WIDTH, 128), HEAD_WIDTH)

    def operand(own_ref, store, i, h, j):
        if isinstance(j, int) and j == 2:
            return own_ref[:, head_cols(i, h)]
        return store[i, j, :, h * HEAD_WIDTH : (h + 1) * HEAD_WIDTH]

    def tile_stats(i, h, j):
        held = lax.rem(i, LAG_LAST + 1)
        scores = scaling * lax.dot_general(
            k[:, head_cols(i, h)], operand(q, hq, i, h, j), NT, preferred_element_type=F32
        )
        dprobs = lax.dot_general(
            v[:, head_cols(i, h)], operand(g, hg, i, h, j), NT, preferred_element_type=F32
        )
        top = jnp.max(scores, axis=0, keepdims=True)
        grown = jnp.exp(scores - top)
        es[held, h, j] = grown
        ds[held, h, j] = dprobs
        st[j, i, h : h + 1, :] = top
        st[j, i, heads + h : heads + h + 1, :] = jnp.sum(grown, axis=0, keepdims=True)
        st[j, i, 2 * heads + h : 2 * heads + h + 1, :] = jnp.sum(grown * dprobs, axis=0, keepdims=True)

    def arrive(i):
        for a in (0, 1):
            for flow in (0, 1):
                halo(flow, i, a, True).wait_recv()
            halo(3, i, a).start()

    def first_tiles(i):
        for a in (0, 1):
            halo(2, i, a, True).wait_recv()
        for h in range(heads):
            for j in (2, 0, 4, 3 - 2 * parity):
                tile_stats(i, h, j)

    def last_tiles(i):
        for a in (0, 1):
            halo(3, i, a, True).wait_recv()
        for h in range(heads):
            tile_stats(i, h, 1 + 2 * parity)
        for j in OTHERS:
            stat_copy(j, i).start()

    def combine(i):
        for j in OTHERS:
            stat_copy(j, i).wait_recv()
        tops, totals, sums, dead = [], [], [], []
        for j in range(WINDOW):
            part = st if j == 2 else rs
            closed = jnp.concatenate(
                [shut[j, pl.ds(piece(i) * heads + h, 1), :] for h in range(heads)], axis=0
            )
            dead.append(closed < 0)
            tops.append(part[j, i, 0:heads, :] + closed)
            totals.append(part[j, i, heads : 2 * heads, :])
            sums.append(part[j, i, 2 * heads : 3 * heads, :])
        top = functools.reduce(jnp.maximum, tops)
        weights = [jnp.exp(t - top) for t in tops]
        total = sum(w * t for w, t in zip(weights, totals))
        delta = sum(w * t for w, t in zip(weights, sums)) / total
        level = top + jnp.log(total)
        for j in range(WINDOW):
            fo[j, i, 0:heads, :] = jnp.where(dead[j], HUGE, level)
            fo[j, i, heads : 2 * heads, :] = delta
        for j in OTHERS:
            final_copy(j, i).start()

    def second_pass(i):
        held = lax.rem(i, LAG_LAST + 1)
        for j in OTHERS:
            final_copy(j, i).wait_recv()
        for h in range(heads):
            key_sum = jnp.zeros((BLK, HEAD_WIDTH), F32)
            value_sum = jnp.zeros((BLK, HEAD_WIDTH), F32)
            for j in range(WINDOW):
                final = fo if j == 2 else fr
                factor = jnp.exp(st[j, i, h : h + 1, :] - final[j, i, h : h + 1, :])
                probs = es[held, h, j] * factor
                score_grad = (probs * (ds[held, h, j] - final[j, i, heads + h : heads + h + 1, :])).astype(BF16)
                value_sum += lax.dot_general(
                    probs.astype(BF16), operand(g, hg, i, h, j), NN, preferred_element_type=F32
                )
                key_sum += lax.dot_general(
                    score_grad, operand(q, hq, i, h, j), NN, preferred_element_type=F32
                )
            key_out = (key_sum * scaling).astype(BF16)
            value_out = value_sum.astype(BF16)
            dk[:, head_cols(i, h)] = key_out
            dv[:, head_cols(i, h)] = value_out
            key_term = lax.dot_general(key_out, wide[...], TN, preferred_element_type=F32)
            value_term = lax.dot_general(value_out, wide[...], TN, preferred_element_type=F32)
            side = lax.broadcasted_iota(jnp.int32, key_term.shape, 1)
            term = jnp.where(side < ka.shape[0], key_term, value_term)
            own[h * HEAD_WIDTH : (h + 1) * HEAD_WIDTH, :] = term
        for a in (0, 1):
            out_copy(i, a).start()

        @pl.when(i >= 2)
        def _():
            z_copy(i - 2).wait_recv()
            own[...] += zr[i - 2].astype(F32)

        @pl.when(i < planes - 1)
        def _():
            zs[i] = own[...].astype(BF16)
            z_copy(i).start()

    @pl.loop(0, planes + LAG_LAST)
    def _(t):
        @pl.when(t < planes)
        def _():
            arrive(t)

        @pl.when(t < planes - AHEAD)
        def _():
            send_halo(t + AHEAD)

        @pl.when(t < planes)
        def _():
            first_tiles(t)

        @pl.when((t >= LAG_STATS) & (t < planes + LAG_STATS))
        def _():
            combine(t - LAG_STATS)

        @pl.when(t >= LAG_LAST)
        def _():
            second_pass(t - LAG_LAST)

        @pl.when(t < planes)
        def _():
            last_tiles(t)

    z_copy(planes - 2).wait_recv()
    own[...] += zr[planes - 2].astype(F32)
    own16[...] = own[...].astype(BF16)
    for d in range(1, x_count):
        x_copy(d).start()
    mine = own[pl.ds(pl.multiple_of(x_at * x_rows, 8), x_rows), :]
    for d in range(1, x_count):
        x_copy(d).wait_recv()
        mine += xr[d - 1].astype(F32)
    rows[...] = mine
    ub[...] = jnp.zeros_like(ub)
    for n in range(group):
        ub[n, 0:y_rows, :] = rows[n * y_rows : (n + 1) * y_rows, :]
    for d in range(1, group):
        y_copy(d).start()
    last = ub[y_at]
    for d in range(1, group):
        y_copy(d).wait_recv()
        last += yr[d - 1]
    ad[...] = last

    @pl.loop(0, planes)
    def _(i):
        for flow in range(4):
            for a in (0, 1):
                halo(flow, i, a).wait_send()
        for a in (0, 1):
            out_copy(i, a).wait()
        for j in OTHERS:
            stat_copy(j, i).wait_send()
            final_copy(j, i).wait_send()

    for i in range(planes - 1):
        z_copy(i).wait_send()
    for d in range(1, x_count):
        x_copy(d).wait_send()
    for d in range(1, group):
        y_copy(d).wait_send()


def finish(parts, part, dk, dv, ad, dk_out, dv_out, ka_grad, va_grad, hold, in_sem, out_sem):
    ins, outs = [], []
    for n in range(parts):
        cols = pl.ds(n * part, part)
        for a, (src, dst) in enumerate(((dk, dk_out), (dv, dv_out))):
            ins.append(pltpu.make_async_copy(src.at[:, cols], hold.at[a, n], in_sem.at[a, n]))
            outs.append(pltpu.make_async_copy(hold.at[a, n], dst.at[:, cols], out_sem.at[a, n]))
    for load in ins:
        load.start()
    rank = ka_grad.shape[1]
    ka_grad[...] = ad[0 : ka_grad.shape[0], 0:rank]
    va_grad[...] = ad[0 : ka_grad.shape[0], rank:]
    for load, store in zip(ins, outs):
        load.wait()
        store.start()
    for store in outs:
        store.wait()


def body(planes, ring, group, hq, hk, hv, og, ka, va, lists, counts):
    head_count = lists.shape[0]
    heads = head_count // planes
    width = heads * HEAD_WIDTH
    rank = ka.shape[-1]
    x_count = ring // group
    x_rows = width // x_count
    y_rows = x_rows // group
    y_pad = -(-y_rows // 8) * 8
    tokens, columns = hq.shape[1:]
    sems = pltpu.SemaphoreType.DMA
    dk, dv, ad = pl.pallas_call(
        functools.partial(kernel, planes, ring, heads, group),
        out_shape=(
            jax.ShapeDtypeStruct((tokens, columns), BF16),
            jax.ShapeDtypeStruct((tokens, columns), BF16),
            jax.ShapeDtypeStruct((y_pad, 2 * rank), F32),
        ),
        in_specs=[pl.BlockSpec(memory_space=pl.ANY)] * 4
        + [pl.BlockSpec(memory_space=pltpu.VMEM)] * 4,
        out_specs=[pl.BlockSpec(memory_space=pl.ANY)] * 2
        + [pl.BlockSpec(memory_space=pltpu.VMEM)],
        scratch_shapes=[
            *[pltpu.VMEM((tokens, columns), BF16)] * 6,
            pltpu.VMEM((tokens, 2 * rank), BF16),
            pltpu.VMEM((WINDOW, head_count, BLK), F32),
            pltpu.VMEM((planes, WINDOW, BLK, width), BF16),
            pltpu.VMEM((planes, WINDOW, BLK, width), BF16),
            pltpu.VMEM((LAG_LAST + 1, heads, WINDOW, BLK, BLK), F32),
            pltpu.VMEM((LAG_LAST + 1, heads, WINDOW, BLK, BLK), F32),
            pltpu.VMEM((WINDOW, planes, 16, BLK), F32),
            pltpu.VMEM((WINDOW, planes, 16, BLK), F32),
            pltpu.VMEM((WINDOW, planes, 8, BLK), F32),
            pltpu.VMEM((WINDOW, planes, 8, BLK), F32),
            pltpu.VMEM((max(planes - 1, 1), width, 2 * rank), BF16),
            pltpu.VMEM((max(planes - 1, 1), width, 2 * rank), BF16),
            pltpu.VMEM((width, 2 * rank), F32),
            pltpu.VMEM((width, 2 * rank), BF16),
            pltpu.VMEM((max(x_count - 1, 1), x_rows, 2 * rank), BF16),
            pltpu.VMEM((x_rows, 2 * rank), F32),
            pltpu.VMEM((group, y_pad, 2 * rank), F32),
            pltpu.VMEM((group - 1, y_pad, 2 * rank), F32),
            sems((4,)),
            sems((planes, 2)),
            sems((4, planes, 2)),
            sems((4, planes, 2)),
            sems((WINDOW, planes)),
            sems((WINDOW, planes)),
            sems((WINDOW, planes)),
            sems((WINDOW, planes)),
            sems((max(planes - 1, 1),)),
            sems((max(planes - 1, 1),)),
            sems((max(x_count - 1, 1),)),
            sems((max(x_count - 1, 1),)),
            sems((group - 1,)),
            sems((group - 1,)),
        ],
        compiler_params=pltpu.CompilerParams(
            collective_id=0, has_side_effects=True, vmem_limit_bytes=60 * 1024 * 1024
        ),
    )(hq[0], hk[0], hv[0], og[0], ka[0].T, va[0].T, lists.transpose(2, 0, 1), counts)
    parts = 4
    part = columns // parts
    dk, dv, ka_grad, va_grad = pl.pallas_call(
        functools.partial(finish, parts, part),
        out_shape=(
            jax.ShapeDtypeStruct((tokens, columns), BF16),
            jax.ShapeDtypeStruct((tokens, columns), BF16),
            jax.ShapeDtypeStruct((y_rows, rank), F32),
            jax.ShapeDtypeStruct((y_rows, rank), F32),
        ),
        in_specs=[pl.BlockSpec(memory_space=pl.ANY)] * 2
        + [pl.BlockSpec(memory_space=pltpu.VMEM)],
        out_specs=[pl.BlockSpec(memory_space=pl.ANY)] * 2
        + [pl.BlockSpec(memory_space=pltpu.VMEM)] * 2,
        scratch_shapes=[
            pltpu.VMEM((2, parts, tokens, part), BF16),
            sems((2, parts)),
            sems((2, parts)),
        ],
    )(dk, dv, ad)
    return dk[None], dv[None], ka_grad, va_grad


def solution(mesh, group=ROW_GROUP):
    split = P("dp", "seq", None)
    rows = P(("dp", "seq"), None)
    return jax.shard_map(
        functools.partial(body, mesh.shape["dp"], mesh.shape["seq"], group),
        mesh=mesh,
        in_specs=(split,) * 6 + (P(), P()),
        out_specs=(split, split, rows, rows),
        check_vma=False,
    )
```
